32 devices in a mesh: rep: 2 (over x), atom: 16 (over z, y, core).
Axes of the slice: x: 2, y: 2, z: 4, core: 2. Of those that a mesh axis runs over, the one named last changes fastest.
Arguments:
- features: bfloat16 [4096, 256], P(('rep', 'atom')), parts along dimension 0, may hold values from -6 to 6
- fractional: float32 [3, 4096], P(None, ('rep', 'atom')), parts along dimension 1, may hold values from 0 to 1, as said below
- distances: float32 [64, 4096], P(None, ('rep', 'atom')), parts along dimension 1, may hold values from 0.8 to 4.8
- neighbours: int32 [64, 4096], P(None, ('rep', 'atom')), parts along dimension 1, may hold values from 0 to 383
- edge_mask: int32 [64, 4096], P(None, ('rep', 'atom')), parts along dimension 1, may hold values 0 or 1
- wave_index: int32 [3, 2048], replicated, may hold values from -6 to 6
- w_rbf: bfloat16 [2, 64, 512], replicated, may hold values from -1.5 to 1.5
- w_filter: bfloat16 [2, 512, 256], replicated, may hold values from -0.25 to 0.25
- w_mixing: bfloat16 [2, 256, 256], replicated, may hold values from -0.375 to 0.375
- w_short: bfloat16 [2, 256, 256], replicated, may hold values from -0.375 to 0.375
- w_long: bfloat16 [2, 256, 256], replicated, may hold values from -0.375 to 0.375
Outputs:
- features_out: bfloat16 [4096, 256], P(('rep', 'atom')), parts along dimension 0
The draws below stay inside these ranges and needn't reach their ends.
There are 2 independent parts, one for each index of `rep`. The reference program is written for one: setup_inputs(seed, part) draws one part's arguments, and reference() takes and returns one part's arrays. A program takes and returns all parts, laid end to end along the dimension named above; an argument that names none is the same for every part. Nothing has to cross between parts.
Inputs may be any that keep to these rules, and one draw needn't show every extreme that they name: neighbours[n, i] indexes the concatenation of the previous brick, atom i's own brick and the next brick, cyclic over the 16 bricks. `fractional`: atom i has its z coordinate within brick i // 128, that is between (i // 128) * 128 / 2048 and one brick further.
All inputs are finite; a program needn't handle non-finite values. No bound on the sum of `edge_mask` on one device may be relied on, other than what follows from the above.
Results may differ from the reference program's by a relative error of at most 0.01.
Values may be sent and summed in bfloat16 or wider, within the bound.
A program may use at most 64 MiB of HBM per device.

```python
import math
import jax
import jax.numpy as jnp
from jax import lax

F = 256
H = 512
R = 64
K = 2048
NB = 64
LAYERS = 2
ATOM_DEV = 128
ATOMS = 2048


def draw_fractional(key, part):
    base = jax.random.fold_in(key, 7)
    first, second = jax.random.split(base)
    plane = jax.random.uniform(first, (2, ATOMS), jnp.float32)
    offset = jax.random.uniform(second, (ATOMS,), jnp.float32)
    brick = (jnp.arange(ATOMS) // ATOM_DEV).astype(jnp.float32)
    height = (brick + offset) * (ATOM_DEV / ATOMS)
    return jnp.concatenate([plane, height[None, :]], axis=0)


def with_ends(result, stream_key, least, high):
    dims = result.shape
    spot = [jax.random.randint(jax.random.fold_in(stream_key, axis), (), 0, dims[axis]) for axis in range(len(dims))]
    result = result.at[tuple(spot)].set(least)
    longest = dims.index(max(dims))
    spot[longest] = (spot[longest] + 1) % dims[longest]
    return result.at[tuple(spot)].set(high)


def block_scale(key, extent, cuts, low, largest):
    gain = 1.0
    for axis_at, parts in cuts:
        heights = jax.random.uniform(jax.random.fold_in(jax.random.fold_in(key, 6), axis_at), (parts,), jnp.float32, low / len(cuts), largest / len(cuts))
        gain = gain * jnp.repeat(jnp.exp(heights), extent[axis_at] // parts).reshape((-1,) + (1,) * (len(extent) - 1 - axis_at))
    return gain


def scatter_about(key, extent, scale, limit, cuts=(), held_as=jnp.bfloat16):
    drawn = jax.random.normal(key, extent, jnp.float32) * scale
    if len(cuts) > 0:
        drawn = block_scale(key, extent, cuts, -0.22, 0.18) * drawn
    return jnp.clip(drawn, min=-limit, max=limit).astype(held_as)


def setup_inputs(seed: int = 0, part: int = 0) -> dict:
    seeds = jax.random.split(jax.random.key(seed), 12)
    own_keys = jax.random.split(jax.random.fold_in(seeds[11], part), 12)
    return {
        "features": scatter_about(own_keys[0], (ATOMS, F), 1.0, 6.0, ((0, 16),)),
        "fractional": draw_fractional(jax.random.fold_in(jax.random.fold_in(seeds[11], part), 71), part),
        "distances": jnp.clip(0.8 + 4 * jax.random.uniform(own_keys[2], (NB, ATOMS), jnp.float32) ** block_scale(own_keys[2], (NB, ATOMS), ((1, 16),), -0.2, 0.2), 0.8, 4.8),
        "neighbours": with_ends(jax.random.randint(own_keys[3], (NB, ATOMS), 0, 3 * ATOM_DEV), jax.random.fold_in(own_keys[3], 1), 0, (3 * ATOM_DEV) - 1).astype(jnp.int32),
        "edge_mask": with_ends((jax.random.randint(own_keys[4], (NB, ATOMS), 0, 4) < 3).astype(jnp.int32), jax.random.fold_in(own_keys[4], 1), 0, 1),
        "wave_index": with_ends(jax.random.randint(seeds[5], (3, K), -6, 7), jax.random.fold_in(seeds[5], 1), -6, 6).astype(jnp.int32),
        "w_rbf": scatter_about(seeds[6], (LAYERS, R, H), (R // 4) ** -0.5, 1.5),
        "w_filter": scatter_about(seeds[7], (LAYERS, H, F), H ** -0.5, 0.25),
        "w_mixing": scatter_about(seeds[8], (LAYERS, F, F), F ** -0.5, 0.375),
        "w_short": scatter_about(seeds[9], (LAYERS, F, F), F ** -0.5, 0.375),
        "w_long": scatter_about(seeds[10], (LAYERS, F, F), F ** -0.5, 0.375),
    }


slot_group = 8
tau_value = 2.0 * math.pi

def edge_basis(distance, count):
    centers = 0.5 + 4.5 * jnp.arange(count, dtype=jnp.float32) / (count - 1)
    offset = distance[..., None] - centers
    return jnp.exp(-4.0 * offset * offset).astype(jnp.bfloat16)

def envelope(distance):
    return 0.5 * (jnp.cos(math.pi * distance / 5.0) + 1.0)

def messages(table, index, distance, edge_weight, rbf_weight, filter_weight):
    groups = index.shape[0] // slot_group
    rows = index.shape[1]
    count = rbf_weight.shape[0]

    def advance(total, pieces):
        index_part, distance_part, weight_part = pieces
        basis = edge_basis(distance_part, count).reshape(slot_group * rows, count)
        inner = jax.nn.silu(jnp.dot(basis, rbf_weight, preferred_element_type=jnp.float32)).astype(jnp.bfloat16)
        filters = jnp.dot(inner, filter_weight, preferred_element_type=jnp.float32).reshape(slot_group, rows, -1)
        filters = filters * weight_part[:, :, None]
        gathered = jnp.take(table, index_part, axis=0).astype(jnp.float32)
        return (total + lax.optimization_barrier(jnp.sum(filters * gathered, axis=0)), None)
    start = jnp.zeros((rows, filter_weight.shape[1]), jnp.float32)
    total, _ = lax.scan(advance, start, (index.reshape(groups, slot_group, rows), distance.reshape(groups, slot_group, rows), edge_weight.reshape(groups, slot_group, rows)))
    return total

def transposed(left, right):
    return lax.dot_general(left, right, (((0,), (0,)), ((), ())), preferred_element_type=jnp.float32)

def reference(features, fractional, distances, neighbours, edge_mask, wave_index, w_rbf, w_filter, w_mixing, w_short, w_long):
    atoms_all = features.shape[0]
    width = features.shape[1]
    brick_start = (jnp.arange(atoms_all, dtype=jnp.int32) // ATOM_DEV * ATOM_DEV).astype(jnp.int32)
    partner = ((brick_start[None, :] - ATOM_DEV + neighbours) % atoms_all).astype(jnp.int32)
    edge_weight = envelope(distances) * edge_mask.astype(jnp.float32)
    wave_float = wave_index.astype(jnp.float32)
    angle = tau_value * (fractional[0][:, None] * wave_float[0][None, :] + fractional[1][:, None] * wave_float[1][None, :] + fractional[2][:, None] * wave_float[2][None, :])
    cosine = jnp.cos(angle).astype(jnp.bfloat16)
    sine = jnp.sin(angle).astype(jnp.bfloat16)
    gains = 1.0 / (1.0 + (wave_float[0] * wave_float[0] + wave_float[1] * wave_float[1] + wave_float[2] * wave_float[2]) / 16.0)
    state = features
    for layer_index in range(LAYERS):
        message = messages(state, partner, distances, edge_weight, w_rbf[layer_index], w_filter[layer_index]).astype(jnp.bfloat16)
        structure = jnp.concatenate([transposed(cosine, state), transposed(sine, state)], axis=1)
        scaled = (structure * gains[:, None] / jnp.sqrt(jnp.float32(atoms_all))).astype(jnp.bfloat16)
        waves = scaled.shape[0]
        potential = jnp.dot(scaled.reshape(2 * waves, width), w_mixing[layer_index], preferred_element_type=jnp.float32)
        potential = potential.reshape(waves, 2 * width).astype(jnp.bfloat16)
        field = jnp.dot(cosine, potential[:, :width], preferred_element_type=jnp.float32)
        field = field + jnp.dot(sine, potential[:, width:], preferred_element_type=jnp.float32)
        field = (field * (4.0 / math.sqrt(K))).astype(jnp.bfloat16)
        update = jnp.dot(message, w_short[layer_index], preferred_element_type=jnp.float32)
        update = update + jnp.dot(field, w_long[layer_index], preferred_element_type=jnp.float32)
        state = (state.astype(jnp.float32) + jax.nn.silu(update)).astype(jnp.bfloat16)
    return state
```

```python
import functools
import math

import jax
import jax.numpy as jnp
import numpy as np
from jax import lax
from jax.experimental import pallas as pl
from jax.experimental.pallas import tpu as pltpu
from jax.sharding import PartitionSpec as P

MOST = 6
STEPS = 8
Z_ROWS = 16


def half_plane():
    pairs = [(0, m1) for m1 in range(MOST + 1)]
    pairs += [(m0, m1) for m0 in range(1, MOST + 1) for m1 in range(-MOST, MOST + 1)]
    return pairs + [(0, 0)] * (-len(pairs) % STEPS)


PAIRS = half_plane()


def row_weights(wave_index, atoms_all):
    m0, m1, m2 = wave_index[0], wave_index[1], wave_index[2]
    flip = (m0 < 0) | ((m0 == 0) & (m1 < 0))
    sign = jnp.where(flip, -1, 1)
    m0, m1, m2 = sign * m0, sign * m1, sign * m2
    pair = jnp.where(m0 == 0, m1, (MOST + 1) + (m0 - 1) * (2 * MOST + 1) + m1 + MOST)
    one_pair = (pair[None, :] == jnp.arange(len(PAIRS))[:, None]).astype(jnp.bfloat16)
    one_z = ((m2 + Z_ROWS // 2)[None, :] == jnp.arange(Z_ROWS)[:, None]).astype(jnp.bfloat16)
    count = lax.dot_general(
        one_pair, one_z, (((1,), (1,)), ((), ())), preferred_element_type=jnp.float32
    )
    grid = np.array(PAIRS, np.float32)
    z = np.arange(Z_ROWS, dtype=np.float32) - Z_ROWS // 2
    norm = (grid * grid).sum(axis=1)[:, None] + (z * z)[None, :]
    weight = count / (1.0 + norm / 16.0) / math.sqrt(atoms_all)
    return jnp.broadcast_to(weight[:, None, :], (len(PAIRS), 2, Z_ROWS)).reshape(-1, 1)


def filter_kernel(layer, distance_ref, rbf_ref, filter_ref, out_ref, rbf_t, filter_t):
    @pl.when(pl.program_id(0) == 0)
    def _():
        rbf_t[...] = (rbf_ref[...].astype(jnp.float32) * 0.5).T.astype(jnp.bfloat16)
        filter_t[...] = filter_ref[...].astype(jnp.float32).T.astype(jnp.bfloat16)

    count = rbf_ref.shape[0]
    slots, rows = distance_ref.shape
    center = 0.5 + 4.5 * lax.broadcasted_iota(jnp.int32, (count, rows), 0).astype(jnp.float32) / (
        count - 1
    )
    parts = []
    for slot in range(slots):
        offset = distance_ref[slot : slot + 1, :] - center
        parts.append(jnp.exp(-4.0 * offset * offset).astype(jnp.bfloat16))
    basis = jnp.concatenate(parts, axis=1)
    half = jnp.dot(rbf_t[...], basis, preferred_element_type=jnp.float32)
    inner = (half + half * jnp.tanh(half)).astype(jnp.bfloat16)
    out_ref[...] = jnp.dot(filter_t[...], inner, preferred_element_type=jnp.float32).astype(
        jnp.bfloat16
    )


def edge_filters(layer, distances, w_rbf, w_filter):
    slots, rows = distances.shape
    _, count, hidden = w_rbf.shape
    width = w_filter.shape[2]
    group = slots // STEPS
    return pl.pallas_call(
        functools.partial(filter_kernel, layer),
        out_shape=jax.ShapeDtypeStruct((width, slots * rows), jnp.bfloat16),
        grid=(STEPS,),
        in_specs=[
            pl.BlockSpec((group, rows), lambda g: (g, 0)),
            pl.BlockSpec((None, count, hidden), lambda g: (layer, 0, 0)),
            pl.BlockSpec((None, hidden, width), lambda g: (layer, 0, 0)),
        ],
        out_specs=pl.BlockSpec((width, group * rows), lambda g: (0, g)),
        scratch_shapes=[
            pltpu.VMEM((hidden, count), jnp.bfloat16),
            pltpu.VMEM((width, hidden), jnp.bfloat16),
        ],
        cost_estimate=pl.CostEstimate(
            flops=2 * slots * rows * hidden * (256 + width),
            bytes_accessed=2 * slots * rows * width,
            transcendentals=slots * rows * hidden,
        ),
        name="filters",
    )(distances, w_rbf, w_filter)


def wave_kernel(fraction_ref, out_ref, plane_c, plane_s, z_c, z_s):
    step = pl.program_id(0)
    atoms = fraction_ref.shape[1]
    tau = 2.0 * math.pi

    @pl.when(step == 0)
    def _():
        def table(axis, count, first):
            order = lax.broadcasted_iota(jnp.int32, (count, atoms), 0) + first
            turn = fraction_ref[axis : axis + 1, :] * order.astype(jnp.float32)
            turn = (turn - jnp.floor(turn + 0.5)) * tau
            return jnp.cos(turn), jnp.sin(turn)

        cos_x, sin_x = table(0, 8, 0)
        cos_y, sin_y = table(1, 16, -8)
        cos_z, sin_z = table(2, Z_ROWS, -(Z_ROWS // 2))
        z_c[...] = cos_z
        z_s[...] = sin_z
        for at, (m0, m1) in enumerate(PAIRS):
            cx, sx = cos_x[m0 : m0 + 1], sin_x[m0 : m0 + 1]
            cy, sy = cos_y[m1 + 8 : m1 + 9], sin_y[m1 + 8 : m1 + 9]
            plane_c[at // 8, at % 8 : at % 8 + 1, :] = cx * cy - sx * sy
            plane_s[at // 8, at % 8 : at % 8 + 1, :] = sx * cy + cx * sy

    group = len(PAIRS) // STEPS
    for local in range(group):
        at = step * group + local
        c = plane_c[at // 8, pl.ds(at % 8, 1), :]
        s = plane_s[at // 8, pl.ds(at % 8, 1), :]
        row = local * 2 * Z_ROWS
        out_ref[row : row + Z_ROWS, :] = (c * z_c[...] - s * z_s[...]).astype(jnp.bfloat16)
        out_ref[row + Z_ROWS : row + 2 * Z_ROWS, :] = (s * z_c[...] + c * z_s[...]).astype(
            jnp.bfloat16
        )


def waves(fraction):
    atoms = fraction.shape[1]
    rows = len(PAIRS) * 2 * Z_ROWS
    block = rows // STEPS
    return pl.pallas_call(
        wave_kernel,
        out_shape=jax.ShapeDtypeStruct((rows, atoms), jnp.bfloat16),
        grid=(STEPS,),
        in_specs=[pl.BlockSpec(fraction.shape, lambda g: (0, 0))],
        out_specs=pl.BlockSpec((block, atoms), lambda g: (g, 0)),
        scratch_shapes=[
            pltpu.VMEM((len(PAIRS) // 8, 8, atoms), jnp.float32),
            pltpu.VMEM((len(PAIRS) // 8, 8, atoms), jnp.float32),
            pltpu.VMEM((Z_ROWS, atoms), jnp.float32),
            pltpu.VMEM((Z_ROWS, atoms), jnp.float32),
        ],
        cost_estimate=pl.CostEstimate(
            flops=6 * rows * atoms, bytes_accessed=2 * rows * atoms, transcendentals=80 * atoms
        ),
        name="waves",
    )(fraction)


def layer_kernel(
    field_scale,
    brick_ref,
    all_ref,
    before_ref,
    own_ref,
    after_ref,
    distance_ref,
    neighbour_ref,
    mask_ref,
    filters_ref,
    wave_ref,
    wave_own_ref,
    weight_ref,
    mixing_ref,
    short_ref,
    long_ref,
    out_ref,
    table,
    message,
    field,
):
    step = pl.program_id(0)
    rows = own_ref.shape[0]

    @pl.when(step == 0)
    def _():
        for at, ref in enumerate((before_ref, own_ref, after_ref)):
            table[:, at * rows : (at + 1) * rows] = ref[...].astype(jnp.float32).T.astype(jnp.bfloat16)
        message[...] = jnp.zeros_like(message)
        field[...] = jnp.zeros_like(field)

    structure = jnp.dot(wave_ref[...], all_ref[...], preferred_element_type=jnp.float32)
    scaled = (structure * weight_ref[...]).astype(jnp.bfloat16)
    potential = jnp.dot(scaled, mixing_ref[...], preferred_element_type=jnp.float32).astype(jnp.bfloat16)
    field[...] += lax.dot_general(
        wave_own_ref[...],
        potential,
        (((0,), (0,)), ((), ())),
        preferred_element_type=jnp.float32,
    )

    weight = 0.5 * (jnp.cos(math.pi * distance_ref[...] / 5.0) + 1.0)
    weight = weight * mask_ref[...].astype(jnp.float32)
    place = lax.broadcasted_iota(jnp.int32, (3 * rows, rows), 0)
    slots = distance_ref.shape[0]
    picks = []
    for slot in range(slots):
        hit = place == neighbour_ref[slot : slot + 1, :]
        picks.append(jnp.where(hit, weight[slot : slot + 1, :], 0.0).astype(jnp.bfloat16))
    pick = jnp.concatenate(picks, axis=1)
    gathered = jnp.dot(table[...], pick, preferred_element_type=jnp.float32)
    product = gathered * filters_ref[...].astype(jnp.float32)
    total = message[...]
    for slot in range(slots):
        total = total + product[:, slot * rows : (slot + 1) * rows]
    message[...] = total

    @pl.when(step == pl.num_programs(0) - 1)
    def _():
        update = jnp.dot(
            message[...].T.astype(jnp.bfloat16), short_ref[...], preferred_element_type=jnp.float32
        )
        update = update + jnp.dot(
            (field[...] * field_scale).astype(jnp.bfloat16),
            long_ref[...],
            preferred_element_type=jnp.float32,
        )
        state = own_ref[...].astype(jnp.float32) + update * jax.nn.sigmoid(update)
        out_ref[...] = state.astype(jnp.bfloat16)


def layer_update(
    layer, brick, bricks, field_scale, everyone, distances, neighbours, mask, filters, wave, weight,
    w_mixing, w_short, w_long,
):
    atoms, width = everyone.shape
    slots, rows = distances.shape
    group = slots // STEPS
    block = wave.shape[0] // STEPS
    slab = pl.BlockSpec((group, rows), lambda g, b: (g, 0))
    matrix = pl.BlockSpec((None, width, width), lambda g, b: (layer, 0, 0))
    return pl.pallas_call(
        functools.partial(layer_kernel, field_scale),
        out_shape=jax.ShapeDtypeStruct((rows, width), jnp.bfloat16),
        grid_spec=pltpu.PrefetchScalarGridSpec(
            num_scalar_prefetch=1,
            grid=(STEPS,),
            in_specs=[
                pl.BlockSpec((atoms, width), lambda g, b: (0, 0)),
                pl.BlockSpec((rows, width), lambda g, b: (lax.rem(b[0] + bricks - 1, bricks), 0)),
                pl.BlockSpec((rows, width), lambda g, b: (b[0], 0)),
                pl.BlockSpec((rows, width), lambda g, b: (lax.rem(b[0] + 1, bricks), 0)),
                slab,
                slab,
                slab,
                pl.BlockSpec((width, group * rows), lambda g, b: (0, g)),
                pl.BlockSpec((block, atoms), lambda g, b: (g, 0)),
                pl.BlockSpec((block, rows), lambda g, b: (g, b[0])),
                pl.BlockSpec((block, 1), lambda g, b: (g, 0)),
                matrix,
                matrix,
                matrix,
            ],
            out_specs=pl.BlockSpec((rows, width), lambda g, b: (0, 0)),
            scratch_shapes=[
                pltpu.VMEM((width, 3 * rows), jnp.bfloat16),
                pltpu.VMEM((width, rows), jnp.float32),
                pltpu.VMEM((rows, width), jnp.float32),
            ],
        ),
        name="update",
    )(
        brick, everyone, everyone, everyone, everyone, distances, neighbours, mask, filters, wave,
        wave, weight, w_mixing, w_short, w_long,
    )


def per_device(
    features, fractional, distances, neighbours, edge_mask, wave_index,
    w_rbf, w_filter, w_mixing, w_short, w_long,
):
    bricks = lax.axis_size("atom")
    brick = jnp.reshape(lax.axis_index("atom"), (1,)).astype(jnp.int32)
    field_scale = 4.0 / math.sqrt(wave_index.shape[1])
    fraction = lax.all_gather(fractional, "atom", axis=1, tiled=True)
    wave = waves(fraction)
    weight = row_weights(wave_index, features.shape[0] * bricks)
    state = features
    for layer in range(w_rbf.shape[0]):
        slots = distances
        if layer > 0:
            slots, state = lax.optimization_barrier((distances, state))
        everyone = lax.all_gather(state, "atom", axis=0, tiled=True)
        filters = edge_filters(layer, slots, w_rbf, w_filter)
        state = layer_update(
            layer, brick, bricks, field_scale, everyone, distances, neighbours, edge_mask, filters,
            wave, weight, w_mixing, w_short, w_long,
        )
    return state


def solution(mesh):
    split_rows = P(("rep", "atom"), None)
    split_columns = P(None, ("rep", "atom"))
    in_specs = (split_rows,) + (split_columns,) * 4 + (P(),) * 6
    return jax.shard_map(
        per_device, mesh=mesh, in_specs=in_specs, out_specs=split_rows, check_vma=False
    )
```
